32 devices in a mesh: grp: 2 (over x), filt: 8 (over z, y), sky: 2 (over core).
Axes of the slice: x: 2, y: 2, z: 4, core: 2. Of those that a mesh axis runs over, the one named last changes fastest.
Arguments:
- strain: bfloat16 [2, 6, 524288], P(None, 'grp', 'filt'), parts along dimension 1, may hold values from -4 to 4
- templates: bfloat16 [2, 4, 524288], P(None, 'sky', 'filt'), may hold values from -6 to 6
- lengths: int32 [4], P('sky'), may hold values from 131072 to 524288
- antenna: bfloat16 [2, 3, 3072], P(None, None, 'sky'), may hold values from -1 to 1
- delays: int32 [3, 3072], P(None, 'sky'), may hold values from -48 to 48
Outputs:
- peak: float32 [2, 2048, 3072], P('grp', 'filt', 'sky'), parts along dimension 0
The draws below stay inside these ranges and needn't reach their ends.
There are 2 independent parts, one for each index of `grp`. The reference program is written for one: setup_inputs(seed, part) draws one part's arguments, and reference() takes and returns one part's arrays. A program takes and returns all parts, laid end to end along the dimension named above; an argument that names none is the same for every part. Nothing has to cross between parts.
All inputs are finite; a program needn't handle non-finite values.
Results may differ from the reference program's by a relative error of at most 0.018.
Values may be sent and summed in bfloat16 or wider, within the bound.
No kernel may reach another device: no remote copies, remote signals or barrier semaphores. Data moves between devices by JAX's collectives and lax.ppermute only.
A program may use at most 64 MiB of HBM per device.

```python
import math
import jax
import jax.numpy as jnp
from jax import lax

N1 = 2048
N2 = 512
NF = 1048576
NH = 524288
DET = 3
SKY = 3072
DM = 48
KT = 4
K2 = 3
KO = 1


def plant(entries, rng, low, high):
    longest = entries.shape.index(max(entries.shape))
    spots = []
    for shift in (0, 1):
        where = [jax.random.randint(jax.random.fold_in(rng, axis), (), 0, length) for axis, length in enumerate(entries.shape)]
        where[longest] = (where[longest] + shift) % entries.shape[longest]
        spots.append(tuple(where))
    return entries.at[spots[0]].set(low).at[spots[1]].set(high)


def steps_of(own_key, extent, pieces, low, top_value):
    def one(position, parts):
        draws = jax.random.uniform(jax.random.fold_in(jax.random.fold_in(own_key, 6), position), (parts,), jnp.float32, low / len(pieces), top_value / len(pieces))
        return jnp.repeat(jnp.exp(draws), extent[position] // parts).reshape((-1,) + (1,) * (len(extent) - position - 1))

    loudness = one(*pieces[0])
    for cut in pieces[1:]:
        loudness = loudness * one(*cut)
    return loudness


def bell_draw(key, extent, deviation, bound, cuts=(), kind=jnp.bfloat16):
    gain = steps_of(key, extent, cuts, -0.22, 0.18) if cuts else 1.0
    values = jax.random.normal(key, extent, jnp.float32) * deviation * gain
    return jnp.minimum(jnp.maximum(values, -bound), bound).astype(kind)


def setup_inputs(seed: int = 0, part: int = 0) -> dict:
    seeds = jax.random.split(jax.random.key(seed), 6)
    part_keys = jax.random.split(jax.random.fold_in(seeds[5], part), 6)
    strain = bell_draw(part_keys[0], (2, DET, NH), 0.5, 4.0, ((2, 8),))
    templates = bell_draw(seeds[1], (2, KT, NH), 1.0, 6.0, ((1, 2), (2, 8)))
    lengths = plant(jax.random.randint(seeds[2], (KT,), NH // 4, NH + 1), jax.random.fold_in(seeds[2], 1), NH // 4, NH).astype(jnp.int32)
    antenna = jnp.clip(jax.random.uniform(seeds[3], (2, DET, SKY), jnp.float32, -1.0, 1.0) * steps_of(seeds[3], (2, DET, SKY), ((2, 2),), -0.4, 0.0), -1.0, 1.0).astype(jnp.bfloat16)
    delays = plant(jax.random.randint(seeds[4], (DET, SKY), -DM, DM + 1), jax.random.fold_in(seeds[4], 1), -DM, DM).astype(jnp.int32)
    return {"strain": strain, "templates": templates, "lengths": lengths, "antenna": antenna, "delays": delays}


TWO_PI = 6.283185307179586

def rounded(values):
    return lax.optimization_barrier(values.astype(jnp.bfloat16)).astype(jnp.float32)

def pick_row(series_row, index_rows):
    return series_row[index_rows]

def reference(strain, templates, lengths, antenna, delays):
    s_re = strain[0].astype(jnp.float32)
    s_im = strain[1].astype(jnp.float32)
    h_re = templates[0].astype(jnp.float32)
    h_im = templates[1].astype(jnp.float32)
    bin_ids = jnp.arange(NH, dtype=jnp.int32)
    in_band = (bin_ids[None, :] < lengths[:, None]).astype(jnp.float32)
    norm2 = lax.optimization_barrier(jnp.sum(in_band * (h_re * h_re + h_im * h_im), axis=1))
    x_re = rounded((h_re[:, None] * s_re[None] + h_im[:, None] * s_im[None]) * in_band[:, None])
    x_im = rounded((h_re[:, None] * s_im[None] - h_im[:, None] * s_re[None]) * in_band[:, None])
    spectrum = (x_re + 1j * x_im).reshape(KT, DET, N1 // 2, N2)
    sectioned = jnp.fft.ifft(spectrum, n=N1, axis=2) * N1
    t_first = jnp.arange(N1, dtype=jnp.int32)
    b_ids = jnp.arange(N2, dtype=jnp.int32)
    angle = (t_first[:, None] * b_ids[None, :]).astype(jnp.float32) * (TWO_PI / NF)
    cos_w = jnp.cos(angle)
    sin_w = jnp.sin(angle)
    y_re = rounded(sectioned.real * cos_w - sectioned.imag * sin_w)
    y_im = rounded(sectioned.real * sin_w + sectioned.imag * cos_w)
    t_second = jnp.arange(K2, dtype=jnp.int32)
    angle_two = (b_ids[:, None] * t_second[None, :]).astype(jnp.float32) * (TWO_PI / N2)
    cos_two = jnp.cos(angle_two)
    sin_two = jnp.sin(angle_two)
    highest = lax.Precision.HIGHEST
    z_re = jnp.einsum('kdab,bc->kdac', y_re, cos_two, precision=highest) - jnp.einsum('kdab,bc->kdac', y_im, sin_two, precision=highest)
    z_im = jnp.einsum('kdab,bc->kdac', y_re, sin_two, precision=highest) + jnp.einsum('kdab,bc->kdac', y_im, cos_two, precision=highest)
    scale = lax.rsqrt(norm2 + 1e-06)[:, None, None, None]
    zn_re = rounded(z_re * scale).transpose(0, 1, 3, 2).reshape(KT, DET, K2 * N1)
    zn_im = rounded(z_im * scale).transpose(0, 1, 3, 2).reshape(KT, DET, K2 * N1)
    sky_block = math.gcd(SKY, 256)
    block_count = SKY // sky_block
    weight_blocks = antenna.astype(jnp.float32).reshape(2, DET, block_count, sky_block).transpose(2, 0, 1, 3)
    delay_blocks = delays.reshape(DET, block_count, sky_block).transpose(1, 0, 2)
    times = N1 + jnp.arange(KO * N1, dtype=jnp.int32)

    def per_block(pair):
        weights, lags = pair
        where_ids = (times[None, None, :] + lags[:, :, None]).astype(jnp.int32)

        def per_template(best, series):
            series_re, series_im = series
            sel_re = jax.vmap(pick_row)(series_re, where_ids)
            sel_im = jax.vmap(pick_row)(series_im, where_ids)
            mix_re = jnp.einsum('pds,dst->pst', weights, sel_re, precision=highest)
            mix_im = jnp.einsum('pds,dst->pst', weights, sel_im, precision=highest)
            power = lax.optimization_barrier(jnp.sum(mix_re * mix_re + mix_im * mix_im, axis=0))
            return (jnp.maximum(best, power), None)
        start = jnp.zeros((sky_block, KO * N1), zn_re.dtype)
        best, unused = lax.scan(per_template, start, (zn_re, zn_im))
        return best
    result = lax.map(per_block, (weight_blocks, delay_blocks))
    return result.reshape(SKY, KO, N1).transpose(1, 2, 0)
```

```python
import functools

import jax
import jax.numpy as jnp
import numpy as np
from jax import lax
from jax.experimental import pallas as pl
from jax.experimental.pallas import tpu as pltpu
from jax.sharding import PartitionSpec as P

N1 = 2048
N2 = 512
DM = 48
K2 = 3
LANES = 128
ROWS = 16


def turn(phase):
    angle = 2.0 * np.pi * (phase - np.floor(phase))
    return np.stack([np.cos(angle), np.sin(angle)]).astype(np.float32)


def tables(depth, rows, whole_length, half_tiles, devices):
    centre2 = 2 * (2 * N1 + DM) - 2 * half_tiles * LANES - 1
    row = np.arange(rows, dtype=np.int64)[:, None]
    col = np.arange(depth, dtype=np.int64)[None, :]
    odd = 2 * np.arange(LANES, dtype=np.int64)[None, :] + 1
    turns = 2 * whole_length
    start = turn(((row * depth + col) * centre2 % turns) / turns)
    col_first = turn((col.T * odd % turns) / turns)
    col_step = turn((col.T * (2 * LANES) % turns) / turns * np.ones((1, LANES)))
    row_first = turn((row * depth * odd % turns) / turns)
    row_step = turn((row * depth * (2 * LANES) % turns) / turns * np.ones((1, LANES)))
    pos = np.arange(devices, dtype=np.int64)[:, None]
    t_up = (centre2 + odd) // 2
    t_down = (centre2 - odd) // 2
    base = rows * depth
    up = turn((pos * base * t_up % whole_length) / whole_length)
    down = turn((pos * base * t_down % whole_length) / whole_length)
    offset = np.concatenate([up, down]).transpose(1, 0, 2)
    flip = np.eye(LANES, dtype=np.float32)[::-1]
    return start, col_first, col_step, row_first, row_step, offset, flip


def series_kernel(
    temps, dets, own, devices, copies, half_tiles,
    lengths, strain, templates, start, col_first, col_step, row_first, row_step, offset, flip,
    out, spectra, sums_a, sums_b, col_now, row_now, series,
):
    rows, depth = strain.shape[2], strain.shape[3]
    count = temps * dets
    pos = lax.axis_index("filt")
    chunk = 16
    norms = [jnp.zeros((chunk, depth), jnp.float32) for _ in range(temps)]

    def filter_chunk(step, norms):
        first = pl.multiple_of(step * chunk, chunk)
        here = pl.ds(first, chunk)
        bins = (
            (pos * rows + first) * depth
            + lax.broadcasted_iota(jnp.int32, (chunk, depth), 0) * depth
            + lax.broadcasted_iota(jnp.int32, (chunk, depth), 1)
        )
        s_re = [strain[0, d, here, :].astype(jnp.float32) for d in range(dets)]
        s_im = [strain[1, d, here, :].astype(jnp.float32) for d in range(dets)]
        p_re, p_im = start[0, here, :], start[1, here, :]
        added = []
        for k in range(temps):
            inside = bins < lengths[k]
            h_re = jnp.where(inside, templates[0, k, here, :].astype(jnp.float32), 0.0)
            h_im = jnp.where(inside, templates[1, k, here, :].astype(jnp.float32), 0.0)
            added.append(norms[k] + (h_re * h_re + h_im * h_im))
            g_re = h_re * p_re + h_im * p_im
            g_im = h_re * p_im - h_im * p_re
            for d in range(dets):
                q = k * dets + d
                x_re = g_re * s_re[d] - g_im * s_im[d]
                x_im = g_re * s_im[d] + g_im * s_re[d]
                spectra[pl.ds(pl.multiple_of(q * rows + first, chunk), chunk), :] = x_re.astype(jnp.bfloat16)
                spectra[pl.ds(pl.multiple_of((count + q) * rows + first, chunk), chunk), :] = x_im.astype(
                    jnp.bfloat16
                )
        return added

    norms = lax.fori_loop(0, rows // chunk, filter_chunk, norms)
    high, low = [], []
    for k in range(temps):
        total = jnp.sum(jnp.sum(norms[k], axis=0, keepdims=True), axis=1, keepdims=True)
        total = jnp.broadcast_to(total, (1, LANES))
        first = total.astype(jnp.bfloat16).astype(jnp.float32)
        high.append(first)
        low.append(total - first)
    f_ur, f_ui, f_dr, f_di = (offset[pos, i : i + 1, :] for i in range(4))

    col_now[...] = col_first[...]
    row_now[...] = row_first[...]

    def section(sums):
        c_re, c_im = col_now[0], col_now[1]
        table = jnp.concatenate([c_re, c_im], axis=1).astype(jnp.bfloat16)
        sums[...] = jnp.dot(spectra[...], table, preferred_element_type=jnp.float32)
        d_re, d_im = col_step[0], col_step[1]
        col_now[0] = c_re * d_re - c_im * d_im
        col_now[1] = c_re * d_im + c_im * d_re

    def collect(sums, tile):
        w_re, w_im = row_now[0], row_now[1]
        up_re, up_im, down_re, down_im = [], [], [], []
        for q in range(count):
            top, low_rows = pl.ds(q * rows, rows), pl.ds((count + q) * rows, rows)
            a, d = sums[top, :LANES], sums[top, LANES:]
            e, b = sums[low_rows, :LANES], sums[low_rows, LANES:]
            s1 = jnp.sum(a * w_re - d * w_im, axis=0, keepdims=True)
            s2 = jnp.sum(b * w_re + e * w_im, axis=0, keepdims=True)
            s3 = jnp.sum(e * w_re - b * w_im, axis=0, keepdims=True)
            s4 = jnp.sum(d * w_re + a * w_im, axis=0, keepdims=True)
            r, i = s1 - s2, s3 + s4
            up_re.append(r * f_ur - i * f_ui)
            up_im.append(r * f_ui + i * f_ur)
            r, i = s1 + s2, s3 - s4
            down_re.append(r * f_dr - i * f_di)
            down_im.append(r * f_di + i * f_dr)
        upper = jnp.concatenate(up_re + high + up_im + low, axis=0).astype(jnp.bfloat16)
        lower = jnp.concatenate(down_re + high + down_im + low, axis=0).astype(jnp.bfloat16)
        upper = jnp.dot(upper, flip[...], preferred_element_type=jnp.float32).astype(jnp.bfloat16)
        series[:, pl.ds(pl.multiple_of((half_tiles - 1 - tile) * LANES, LANES), LANES)] = upper
        series[:, pl.ds(pl.multiple_of((half_tiles + tile) * LANES, LANES), LANES)] = lower
        d_re, d_im = row_step[0], row_step[1]
        row_now[0] = w_re * d_re - w_im * d_im
        row_now[1] = w_re * d_im + w_im * d_re

    section(sums_a)

    def pair(step, carry):
        section(sums_b)
        collect(sums_a, 2 * step)
        section(sums_a)
        collect(sums_b, 2 * step + 1)
        return carry

    pairs = (half_tiles - 1) // 2
    lax.fori_loop(0, pairs, pair, 0)
    if half_tiles % 2:
        collect(sums_a, half_tiles - 1)
    else:
        section(sums_b)
        collect(sums_a, half_tiles - 2)
        collect(sums_b, half_tiles - 1)

    width = out.shape[2]
    for target in range(devices):
        first = own * (devices - 1 - target)
        window = series[:, first : first + width]
        for copy in range(copies):
            out[target * copies + copy] = window


def sky_kernel(temps, dets, own, sources, copies, received, delays, antenna, out, hankel, weights):
    width = received.shape[2]
    sky = delays.shape[1]
    tile = 2 * LANES
    lag = DM - lax.broadcasted_iota(jnp.int32, (LANES, sky), 0)
    for d in range(dets):
        hit = lag == delays[d : d + 1, :]
        for p in range(2):
            value = jnp.where(hit, antenna[p, d : d + 1, :].astype(jnp.float32), 0.0).astype(jnp.bfloat16)
            for i in range(sky // tile):
                weights[i, d * LANES : (d + 1) * LANES, p * tile : (p + 1) * tile] = value[:, i * tile : (i + 1) * tile]
    count = temps * dets
    block = min(own, LANES)
    for c in range(copies):
        total = received[c].astype(jnp.float32)
        for source in range(1, sources):
            total = total + received[source * copies + c].astype(jnp.float32)
        scales = []
        for k in range(temps):
            norm = total[count + k : count + k + 1] + total[ROWS // 2 + count + k : ROWS // 2 + count + k + 1]
            scales.append(lax.rsqrt(norm + 1e-06))
        for k in range(temps):
            for part in range(2):
                for d in range(dets):
                    row = part * (ROWS // 2) + k * dets + d
                    line = (total[row : row + 1] * scales[k]).astype(jnp.bfloat16).astype(jnp.float32)
                    for first in range(0, own, block):
                        start = own - block - first
                        piece = jnp.broadcast_to(line[:, start : start + 2 * LANES], (block, 2 * LANES))
                        moved = pltpu.roll(piece, 2 * LANES + 1 - block, 1, stride=1, stride_axis=0)
                        hankel[
                            c * temps + k, part * own + first : part * own + first + block, d * LANES : (d + 1) * LANES
                        ] = moved[:, :LANES].astype(jnp.bfloat16)

    def sky_tile(i, carry):
        best = None
        for k in range(copies * temps):
            mixed = jnp.dot(hankel[k], weights[i], preferred_element_type=jnp.float32)
            power = mixed * mixed
            power = power[:own] + power[own:]
            power = power[:, :tile] + power[:, tile:]
            best = power if best is None else jnp.maximum(best, power)
        out[:, pl.ds(pl.multiple_of(i * tile, tile), tile)] = best
        return carry

    lax.fori_loop(0, sky // tile, sky_tile, 0)


def body(strain, templates, lengths, antenna, delays):
    devices = lax.axis_size("filt")
    copies = lax.axis_size("sky")
    temps, dets, bins = templates.shape[1], strain.shape[1], strain.shape[2]
    sky = delays.shape[1]
    depth = N2
    rows = bins // depth
    whole_length = 2 * bins * devices
    own = N1 // devices
    span = N1 + 2 * DM
    half_tiles = -(-span // (2 * LANES))
    width = -(-own // LANES) * LANES + LANES
    tabs = tables(depth, rows, whole_length, half_tiles, devices)
    start, col_first, col_step, row_first, row_step, offset = (jnp.asarray(t) for t in tabs[:6])
    flip = jnp.asarray(tabs[6], jnp.bfloat16)
    count = temps * dets
    vmem = pl.BlockSpec(memory_space=pltpu.VMEM)
    smem = pl.BlockSpec(memory_space=pltpu.SMEM)
    shaped_s = strain.reshape(2, dets, rows, depth)
    shaped_h = templates.reshape(2, temps, rows, depth)
    parts = pl.pallas_call(
        functools.partial(series_kernel, temps, dets, own, devices, copies, half_tiles),
        out_shape=jax.ShapeDtypeStruct((devices * copies, ROWS, width), jnp.bfloat16),
        in_specs=[smem] + [vmem] * 9,
        out_specs=vmem,
        scratch_shapes=[
            pltpu.VMEM((2 * count * rows, depth), jnp.bfloat16),
            pltpu.VMEM((2 * count * rows, 2 * LANES), jnp.float32),
            pltpu.VMEM((2 * count * rows, 2 * LANES), jnp.float32),
            pltpu.VMEM((2, depth, LANES), jnp.float32),
            pltpu.VMEM((2, rows, LANES), jnp.float32),
            pltpu.VMEM((ROWS, 2 * half_tiles * LANES), jnp.bfloat16),
        ],
        compiler_params=pltpu.CompilerParams(vmem_limit_bytes=48 << 20),
        name="series",
    )(lengths, shaped_s, shaped_h, start, col_first, col_step, row_first, row_step, offset, flip)
    received = lax.all_to_all(parts, ("filt", "sky"), split_axis=0, concat_axis=0, tiled=True)
    best = pl.pallas_call(
        functools.partial(sky_kernel, temps, dets, own, devices, copies),
        out_shape=jax.ShapeDtypeStruct((own, sky), jnp.float32),
        in_specs=[vmem] * 3,
        out_specs=vmem,
        scratch_shapes=[
            pltpu.VMEM((copies * temps, 2 * own, dets * LANES), jnp.bfloat16),
            pltpu.VMEM((sky // (2 * LANES), dets * LANES, 4 * LANES), jnp.bfloat16),
        ],
        compiler_params=pltpu.CompilerParams(vmem_limit_bytes=48 << 20),
        name="sky",
    )(received, delays, antenna)
    return best[None]


def solution(mesh):
    in_specs = (
        P(None, "grp", "filt"),
        P(None, "sky", "filt"),
        P("sky"),
        P(None, None, "sky"),
        P(None, "sky"),
    )
    out_specs = P("grp", "filt", "sky")
    return jax.shard_map(body, mesh=mesh, in_specs=in_specs, out_specs=out_specs, check_vma=False)
```

```python
import functools

import jax
import jax.numpy as jnp
import numpy as np
from jax import lax
from jax.experimental import pallas as pl
from jax.experimental.pallas import tpu as pltpu
from jax.sharding import PartitionSpec as P

N1 = 2048
N2 = 512
DM = 48
K2 = 3
LANES = 128
ROWS = 16


def turn(phase):
    angle = 2.0 * np.pi * (phase - np.floor(phase))
    return np.stack([np.cos(angle), np.sin(angle)]).astype(np.float32)


def tables(depth, rows, whole_length, half_tiles, devices):
    centre2 = 2 * (2 * N1 + DM) - 2 * half_tiles * LANES - 1
    row = np.arange(rows, dtype=np.int64)[:, None]
    col = np.arange(depth, dtype=np.int64)[None, :]
    odd = 2 * np.arange(LANES, dtype=np.int64)[None, :] + 1
    turns = 2 * whole_length
    start = turn(((row * depth + col) * centre2 % turns) / turns)
    col_first = turn((col.T * odd % turns) / turns)
    col_step = turn((col.T * (2 * LANES) % turns) / turns * np.ones((1, LANES)))
    row_first = turn((row * depth * odd % turns) / turns)
    row_step = turn((row * depth * (2 * LANES) % turns) / turns * np.ones((1, LANES)))
    pos = np.arange(devices, dtype=np.int64)[:, None]
    t_up = (centre2 + odd) // 2
    t_down = (centre2 - odd) // 2
    base = rows * depth
    up = turn((pos * base * t_up % whole_length) / whole_length)
    down = turn((pos * base * t_down % whole_length) / whole_length)
    offset = np.concatenate([up, down]).transpose(1, 0, 2)
    flip = np.eye(LANES, dtype=np.float32)[::-1]
    return start, col_first, col_step, row_first, row_step, offset, flip


def series_kernel(
    temps, dets, own, devices, copies, half_tiles, together,
    lengths, strain, templates, start, col_first, col_step, row_first, row_step, offset, flip,
    out, spectra, col_now, row_now, series,
):
    rows, depth = strain.shape[2], strain.shape[3]
    count = temps * dets
    pos = lax.axis_index("filt")
    norms = [jnp.zeros((ROWS, depth), jnp.float32) for _ in range(temps)]

    def filter_chunk(step, norms):
        first = pl.multiple_of(step * ROWS, ROWS)
        here = pl.ds(first, ROWS)
        bins = (
            (pos * rows + first) * depth
            + lax.broadcasted_iota(jnp.int32, (ROWS, depth), 0) * depth
            + lax.broadcasted_iota(jnp.int32, (ROWS, depth), 1)
        )
        s_re = [strain[0, d, here, :].astype(jnp.float32) for d in range(dets)]
        s_im = [strain[1, d, here, :].astype(jnp.float32) for d in range(dets)]
        p_re, p_im = start[0, here, :], start[1, here, :]
        added = []
        for k in range(temps):
            inside = bins < lengths[k]
            h_re = jnp.where(inside, templates[0, k, here, :].astype(jnp.float32), 0.0)
            h_im = jnp.where(inside, templates[1, k, here, :].astype(jnp.float32), 0.0)
            added.append(norms[k] + (h_re * h_re + h_im * h_im))
            g_re = h_re * p_re + h_im * p_im
            g_im = h_re * p_im - h_im * p_re
            for d in range(dets):
                place = 2 * ((k * dets + d) * rows + first)
                x_re = g_re * s_re[d] - g_im * s_im[d]
                x_im = g_re * s_im[d] + g_im * s_re[d]
                spectra[pl.ds(pl.multiple_of(place, ROWS), ROWS), :] = x_re.astype(jnp.bfloat16)
                spectra[pl.ds(pl.multiple_of(place + ROWS, ROWS), ROWS), :] = x_im.astype(jnp.bfloat16)
        return added

    norms = lax.fori_loop(0, rows // ROWS, filter_chunk, norms)
    high, low = [], []
    for k in range(temps):
        total = jnp.sum(jnp.sum(norms[k], axis=0, keepdims=True), axis=1, keepdims=True)
        total = jnp.broadcast_to(total, (1, LANES))
        first = total.astype(jnp.bfloat16).astype(jnp.float32)
        high.append(first)
        low.append(total - first)
    f_ur, f_ui, f_dr, f_di = (offset[pos, i : i + 1, :] for i in range(4))

    col_now[...] = col_first[...]
    row_now[...] = row_first[...]

    def section(tile):
        c_re, c_im = col_now[0], col_now[1]
        table = jnp.concatenate([c_re, c_im], axis=1).astype(jnp.bfloat16)
        d_re, d_im = col_step[0], col_step[1]
        col_now[0] = c_re * d_re - c_im * d_im
        col_now[1] = c_re * d_im + c_im * d_re
        parts = 2
        height = spectra.shape[0] // parts
        pieces = [
            jnp.dot(spectra[i * height : (i + 1) * height, :], table, preferred_element_type=jnp.float32)
            for i in range(parts)
        ]
        up_re, up_im, down_re, down_im = [], [], [], []
        for q in range(count):
            s1 = s2 = s3 = s4 = None
            for block in range(0, rows, ROWS):
                place = 2 * (q * rows + block)
                for half in range(0, ROWS, 8):
                    w_re = row_now[0, block + half : block + half + 8, :]
                    w_im = row_now[1, block + half : block + half + 8, :]
                    sums = pieces[place // height]
                    top, end = place % height + half, place % height + ROWS + half
                    a, d = sums[top : top + 8, :LANES], sums[top : top + 8, LANES:]
                    e, b = sums[end : end + 8, :LANES], sums[end : end + 8, LANES:]
                    n1, n2 = a * w_re - d * w_im, b * w_re + e * w_im
                    n3, n4 = e * w_re - b * w_im, d * w_re + a * w_im
                    s1 = n1 if s1 is None else s1 + n1
                    s2 = n2 if s2 is None else s2 + n2
                    s3 = n3 if s3 is None else s3 + n3
                    s4 = n4 if s4 is None else s4 + n4
            r = jnp.sum(s1 - s2, axis=0, keepdims=True)
            i = jnp.sum(s3 + s4, axis=0, keepdims=True)
            up_re.append(r * f_ur - i * f_ui)
            up_im.append(r * f_ui + i * f_ur)
            r = jnp.sum(s1 + s2, axis=0, keepdims=True)
            i = jnp.sum(s3 - s4, axis=0, keepdims=True)
            down_re.append(r * f_dr - i * f_di)
            down_im.append(r * f_di + i * f_dr)
        upper = jnp.concatenate(up_re + high + up_im + low, axis=0).astype(jnp.bfloat16)
        lower = jnp.concatenate(down_re + high + down_im + low, axis=0).astype(jnp.bfloat16)
        upper = jnp.dot(upper, flip[...], preferred_element_type=jnp.float32).astype(jnp.bfloat16)
        series[:, pl.ds(pl.multiple_of((half_tiles - 1 - tile) * LANES, LANES), LANES)] = upper
        series[:, pl.ds(pl.multiple_of((half_tiles + tile) * LANES, LANES), LANES)] = lower
        w_re, w_im = row_now[0], row_now[1]
        d_re, d_im = row_step[0], row_step[1]
        row_now[0] = w_re * d_re - w_im * d_im
        row_now[1] = w_re * d_im + w_im * d_re

    def some(step, carry):
        for sub in range(together):
            section(step * together + sub)
        return carry

    lax.fori_loop(0, half_tiles // together, some, 0)

    width = out.shape[2]
    for target in range(devices):
        first = own * (devices - 1 - target)
        window = series[:, first : first + width]
        for copy in range(copies):
            out[target * copies + copy] = window


def weight_kernel(dets, delays, antenna, weights):
    tile = 2 * LANES
    sky = delays.shape[1]
    lag = DM - lax.broadcasted_iota(jnp.int32, (LANES, tile), 0)
    for i in range(sky // tile):
        part = slice(i * tile, (i + 1) * tile)
        for d in range(dets):
            hit = lag == delays[d : d + 1, part]
            for p in range(2):
                value = jnp.where(hit, antenna[p, d : d + 1, part].astype(jnp.float32), 0.0)
                weights[i, d * LANES : (d + 1) * LANES, p * tile : (p + 1) * tile] = value.astype(jnp.bfloat16)


def sky_kernel(temps, dets, own, sources, copies, received, weights, out, hankel):
    width = received.shape[2]
    tile = 2 * LANES
    count = temps * dets
    blocks = -(-own // LANES)
    groups = 2 * copies * temps

    @pl.when(pl.program_id(0) == 0)
    def _():
        for c in range(copies):
            total = received[c].astype(jnp.float32)
            for source in range(1, sources):
                total = total + received[source * copies + c].astype(jnp.float32)
            half = ROWS // 2
            for k in range(temps):
                norm = total[count + k : count + k + 1] + total[half + count + k : half + count + k + 1]
                scale = lax.rsqrt(norm + 1e-06)
                lines = []
                for part in range(2):
                    for d in range(dets):
                        row = part * half + k * dets + d
                        line = (total[row : row + 1] * scale).astype(jnp.bfloat16).astype(jnp.float32)
                        lines.append(
                            pltpu.roll(jnp.broadcast_to(line, (8, width)), 0, 1, stride=1, stride_axis=0)
                        )
                base = jnp.concatenate(lines, axis=0)
                for first in range(0, min(own, LANES), ROWS):
                    moved = [
                        pltpu.roll(base, (t + 1 - own + (blocks - 1) * LANES) % width, 1) for t in (first, first + 8)
                    ]
                    for part in range(2):
                        group = 2 * (c * temps + k) + part
                        for d in range(dets):
                            row = 8 * (part * dets + d)
                            for block in range(blocks):
                                lane = (blocks - 1 - block) * LANES
                                piece = jnp.concatenate([m[row : row + 8, lane : lane + LANES] for m in moved], axis=0)
                                place = ((block * LANES + first) // ROWS * groups + group) * ROWS
                                hankel[place : place + ROWS, d * LANES : (d + 1) * LANES] = piece.astype(jnp.bfloat16)

    span = min(128, own)
    for first in range(0, own, ROWS):
        if first % span == 0:
            mixed = jnp.dot(
                hankel[first * groups : (first + span) * groups, :], weights[0], preferred_element_type=jnp.float32
            )
        best = None
        for k in range(copies * temps):
            place = first % span * groups + 2 * k * ROWS
            re, im = mixed[place : place + ROWS], mixed[place + ROWS : place + 2 * ROWS]
            power = re * re + im * im
            power = power[:, :tile] + power[:, tile:]
            best = power if best is None else jnp.maximum(best, power)
        out[first : first + ROWS, :] = best


def body(strain, templates, lengths, antenna, delays):
    devices = lax.axis_size("filt")
    copies = lax.axis_size("sky")
    temps, dets, bins = templates.shape[1], strain.shape[1], strain.shape[2]
    sky = delays.shape[1]
    depth = N2
    rows = bins // depth
    whole_length = 2 * bins * devices
    own = N1 // devices
    span = N1 + 2 * DM
    half_tiles = -(-span // (2 * LANES))
    width = -(-own // LANES) * LANES + LANES
    tabs = tables(depth, rows, whole_length, half_tiles, devices)
    start, col_first, col_step, row_first, row_step, offset = (jnp.asarray(t) for t in tabs[:6])
    flip = jnp.asarray(tabs[6], jnp.bfloat16)
    count = temps * dets
    vmem = pl.BlockSpec(memory_space=pltpu.VMEM)
    smem = pl.BlockSpec(memory_space=pltpu.SMEM)
    shaped_s = strain.reshape(2, dets, rows, depth)
    shaped_h = templates.reshape(2, temps, rows, depth)
    parts = pl.pallas_call(
        functools.partial(series_kernel, temps, dets, own, devices, copies, half_tiles, 1),
        out_shape=jax.ShapeDtypeStruct((devices * copies, ROWS, width), jnp.bfloat16),
        in_specs=[smem] + [vmem] * 9,
        out_specs=vmem,
        scratch_shapes=[
            pltpu.VMEM((2 * count * rows, depth), jnp.bfloat16),
            pltpu.VMEM((2, depth, LANES), jnp.float32),
            pltpu.VMEM((2, rows, LANES), jnp.float32),
            pltpu.VMEM((ROWS, 2 * half_tiles * LANES), jnp.bfloat16),
        ],
        compiler_params=pltpu.CompilerParams(vmem_limit_bytes=40 << 20),
        name="series",
    )(lengths, shaped_s, shaped_h, start, col_first, col_step, row_first, row_step, offset, flip)
    received = lax.all_to_all(parts, ("filt", "sky"), split_axis=0, concat_axis=0, tiled=True)
    tile = 2 * LANES
    weights = pl.pallas_call(
        functools.partial(weight_kernel, dets),
        out_shape=jax.ShapeDtypeStruct((sky // tile, dets * LANES, 2 * tile), jnp.bfloat16),
        in_specs=[vmem] * 2,
        out_specs=vmem,
        compiler_params=pltpu.CompilerParams(vmem_limit_bytes=16 << 20),
        cost_estimate=pl.CostEstimate(flops=1 << 22, bytes_accessed=3 << 20, transcendentals=0),
        name="weights",
    )(delays, antenna)
    best = pl.pallas_call(
        functools.partial(sky_kernel, temps, dets, own, devices, copies),
        out_shape=jax.ShapeDtypeStruct((own, sky), jnp.float32),
        grid=(sky // tile,),
        in_specs=[vmem, pl.BlockSpec((1, dets * LANES, 2 * tile), lambda i: (i, 0, 0))],
        out_specs=pl.BlockSpec((own, tile), lambda i: (0, i)),
        scratch_shapes=[pltpu.VMEM((copies * temps * 2 * own, dets * LANES), jnp.bfloat16)],
        compiler_params=pltpu.CompilerParams(vmem_limit_bytes=24 << 20),
        name="sky",
    )(received, weights)
    return best[None]


def solution(mesh):
    in_specs = (
        P(None, "grp", "filt"),
        P(None, "sky", "filt"),
        P("sky"),
        P(None, None, "sky"),
        P(None, "sky"),
    )
    out_specs = P("grp", "filt", "sky")
    return jax.shard_map(body, mesh=mesh, in_specs=in_specs, out_specs=out_specs, check_vma=False)
```

```python
import functools

import jax
import jax.numpy as jnp
import numpy as np
from jax import lax
from jax.experimental import pallas as pl
from jax.experimental.pallas import tpu as pltpu
from jax.sharding import PartitionSpec as P

N1 = 2048
N2 = 512
DM = 48
K2 = 3
LANES = 128
ROWS = 16


def turn(phase):
    angle = 2.0 * np.pi * (phase - np.floor(phase))
    return np.stack([np.cos(angle), np.sin(angle)]).astype(np.float32)


def tables(depth, rows, whole_length, half_tiles, devices):
    centre2 = 2 * (2 * N1 + DM) - 2 * half_tiles * LANES - 1
    row = np.arange(rows, dtype=np.int64)[:, None]
    col = np.arange(depth, dtype=np.int64)[None, :]
    odd = 2 * np.arange(LANES, dtype=np.int64)[None, :] + 1
    turns = 2 * whole_length
    start = turn(((row * depth + col) * centre2 % turns) / turns)
    col_first = turn((col.T * odd % turns) / turns)
    col_step = turn((col.T * (2 * LANES) % turns) / turns * np.ones((1, LANES)))
    row_first = turn((row * depth * odd % turns) / turns)
    row_step = turn((row * depth * (2 * LANES) % turns) / turns * np.ones((1, LANES)))
    pos = np.arange(devices, dtype=np.int64)[:, None]
    t_up = (centre2 + odd) // 2
    t_down = (centre2 - odd) // 2
    base = rows * depth
    up = turn((pos * base * t_up % whole_length) / whole_length)
    down = turn((pos * base * t_down % whole_length) / whole_length)
    offset = np.concatenate([up, down]).transpose(1, 0, 2)
    flip = np.eye(LANES, dtype=np.float32)[::-1]
    return start, col_first, col_step, row_first, row_step, offset, flip


def series_kernel(
    temps, dets, own, devices, copies, half_tiles, together,
    lengths, strain, templates, start, col_first, col_step, row_first, row_step, offset, flip,
    out, spectra, col_now, row_now, series,
):
    rows, depth = strain.shape[2], strain.shape[3]
    count = temps * dets
    pos = lax.axis_index("filt")
    norms = [jnp.zeros((ROWS, depth), jnp.float32) for _ in range(temps)]

    def filter_chunk(step, norms):
        first = pl.multiple_of(step * ROWS, ROWS)
        here = pl.ds(first, ROWS)
        bins = (
            (pos * rows + first) * depth
            + lax.broadcasted_iota(jnp.int32, (ROWS, depth), 0) * depth
            + lax.broadcasted_iota(jnp.int32, (ROWS, depth), 1)
        )
        s_re = [strain[0, d, here, :].astype(jnp.float32) for d in range(dets)]
        s_im = [strain[1, d, here, :].astype(jnp.float32) for d in range(dets)]
        p_re, p_im = start[0, here, :], start[1, here, :]
        added = []
        for k in range(temps):
            inside = bins < lengths[k]
            h_re = jnp.where(inside, templates[0, k, here, :].astype(jnp.float32), 0.0)
            h_im = jnp.where(inside, templates[1, k, here, :].astype(jnp.float32), 0.0)
            added.append(norms[k] + (h_re * h_re + h_im * h_im))
            g_re = h_re * p_re + h_im * p_im
            g_im = h_re * p_im - h_im * p_re
            for d in range(dets):
                place = 2 * ((k * dets + d) * rows + first)
                x_re = g_re * s_re[d] - g_im * s_im[d]
                x_im = g_re * s_im[d] + g_im * s_re[d]
                spectra[pl.ds(pl.multiple_of(place, ROWS), ROWS), :] = x_re.astype(jnp.bfloat16)
                spectra[pl.ds(pl.multiple_of(place + ROWS, ROWS), ROWS), :] = x_im.astype(jnp.bfloat16)
        return added

    norms = lax.fori_loop(0, rows // ROWS, filter_chunk, norms)
    high, low = [], []
    for k in range(temps):
        total = jnp.sum(jnp.sum(norms[k], axis=0, keepdims=True), axis=1, keepdims=True)
        total = jnp.broadcast_to(total, (1, LANES))
        first = total.astype(jnp.bfloat16).astype(jnp.float32)
        high.append(first)
        low.append(total - first)
    f_ur, f_ui, f_dr, f_di = (offset[pos, i : i + 1, :] for i in range(4))

    col_now[...] = col_first[...]
    row_now[...] = row_first[...]

    def section(tile):
        c_re, c_im = col_now[0], col_now[1]
        table = jnp.concatenate([c_re, c_im], axis=1).astype(jnp.bfloat16)
        d_re, d_im = col_step[0], col_step[1]
        col_now[0] = c_re * d_re - c_im * d_im
        col_now[1] = c_re * d_im + c_im * d_re
        parts = 2
        height = spectra.shape[0] // parts
        pieces = [
            jnp.dot(spectra[i * height : (i + 1) * height, :], table, preferred_element_type=jnp.float32)
            for i in range(parts)
        ]
        up_re, up_im, down_re, down_im = [], [], [], []
        for q in range(count):
            s1 = s2 = s3 = s4 = None
            for block in range(0, rows, ROWS):
                place = 2 * (q * rows + block)
                for half in range(0, ROWS, 8):
                    w_re = row_now[0, block + half : block + half + 8, :]
                    w_im = row_now[1, block + half : block + half + 8, :]
                    sums = pieces[place // height]
                    top, end = place % height + half, place % height + ROWS + half
                    a, d = sums[top : top + 8, :LANES], sums[top : top + 8, LANES:]
                    e, b = sums[end : end + 8, :LANES], sums[end : end + 8, LANES:]
                    n1, n2 = a * w_re - d * w_im, b * w_re + e * w_im
                    n3, n4 = e * w_re - b * w_im, d * w_re + a * w_im
                    s1 = n1 if s1 is None else s1 + n1
                    s2 = n2 if s2 is None else s2 + n2
                    s3 = n3 if s3 is None else s3 + n3
                    s4 = n4 if s4 is None else s4 + n4
            r = jnp.sum(s1 - s2, axis=0, keepdims=True)
            i = jnp.sum(s3 + s4, axis=0, keepdims=True)
            up_re.append(r * f_ur - i * f_ui)
            up_im.append(r * f_ui + i * f_ur)
            r = jnp.sum(s1 + s2, axis=0, keepdims=True)
            i = jnp.sum(s3 - s4, axis=0, keepdims=True)
            down_re.append(r * f_dr - i * f_di)
            down_im.append(r * f_di + i * f_dr)
        upper = jnp.concatenate(up_re + high + up_im + low, axis=0).astype(jnp.bfloat16)
        lower = jnp.concatenate(down_re + high + down_im + low, axis=0).astype(jnp.bfloat16)
        upper = jnp.dot(upper, flip[...], preferred_element_type=jnp.float32).astype(jnp.bfloat16)
        series[:, pl.ds(pl.multiple_of((half_tiles - 1 - tile) * LANES, LANES), LANES)] = upper
        series[:, pl.ds(pl.multiple_of((half_tiles + tile) * LANES, LANES), LANES)] = lower
        w_re, w_im = row_now[0], row_now[1]
        d_re, d_im = row_step[0], row_step[1]
        row_now[0] = w_re * d_re - w_im * d_im
        row_now[1] = w_re * d_im + w_im * d_re

    def some(step, carry):
        for sub in range(together):
            section(step * together + sub)
        return carry

    lax.fori_loop(0, half_tiles // together, some, 0)

    width = out.shape[2]
    for target in range(devices):
        first = own * (devices - 1 - target)
        window = series[:, first : first + width]
        for copy in range(copies):
            out[target * copies + copy] = window


def weight_kernel(dets, tile, delays, antenna, weights):
    sky = delays.shape[1]
    lag = DM - lax.broadcasted_iota(jnp.int32, (LANES, tile), 0)
    for i in range(sky // tile):
        part = slice(i * tile, (i + 1) * tile)
        rows = [[antenna[p, d : d + 1, part].astype(jnp.float32) for d in range(dets)] for p in range(2)]
        x, y = rows[0][-1], rows[1][-1]
        most = jnp.maximum(jnp.abs(x), jnp.abs(y))
        some = most > 0.0
        least = jnp.where(some, most, 1.0)
        x, y = jnp.where(some, x / least, 1.0), jnp.where(some, y / least, 0.0)
        unit = lax.rsqrt(x * x + y * y)
        cos, sin = x * unit, y * unit
        first = [cos * rows[0][d] + sin * rows[1][d] for d in range(dets)]
        second = [cos * rows[1][d] - sin * rows[0][d] for d in range(dets - 1)]
        for d in range(dets):
            hit = lag == delays[d : d + 1, part]
            weights[i, d * LANES : (d + 1) * LANES, :] = jnp.where(hit, first[d], 0.0).astype(jnp.bfloat16)
            if d < dets - 1:
                place = (dets + d) * LANES
                weights[i, place : place + LANES, :] = jnp.where(hit, second[d], 0.0).astype(jnp.bfloat16)


def sky_kernel(temps, dets, own, sources, copies, received, weights, out, hankel):
    width = received.shape[2]
    count = temps * dets
    blocks = -(-own // LANES)
    groups = 2 * copies * temps

    @pl.when(pl.program_id(0) == 0)
    def _():
        for c in range(copies):
            total = received[c].astype(jnp.float32)
            for source in range(1, sources):
                total = total + received[source * copies + c].astype(jnp.float32)
            half = ROWS // 2
            for k in range(temps):
                norm = total[count + k : count + k + 1] + total[half + count + k : half + count + k + 1]
                scale = lax.rsqrt(norm + 1e-06)
                lines = []
                for part in range(2):
                    for d in range(dets):
                        row = part * half + k * dets + d
                        line = (total[row : row + 1] * scale).astype(jnp.bfloat16).astype(jnp.float32)
                        lines.append(
                            pltpu.roll(jnp.broadcast_to(line, (8, width)), 0, 1, stride=1, stride_axis=0)
                        )
                base = jnp.concatenate(lines, axis=0)
                for first in range(0, min(own, LANES), ROWS):
                    moved = [
                        pltpu.roll(base, (t + 1 - own + (blocks - 1) * LANES) % width, 1) for t in (first, first + 8)
                    ]
                    for part in range(2):
                        group = 2 * (c * temps + k) + part
                        for d in range(dets):
                            row = 8 * (part * dets + d)
                            for block in range(blocks):
                                lane = (blocks - 1 - block) * LANES
                                piece = jnp.concatenate([m[row : row + 8, lane : lane + LANES] for m in moved], axis=0)
                                place = ((block * LANES + first) // ROWS * groups + group) * ROWS
                                hankel[place : place + ROWS, d * LANES : (d + 1) * LANES] = piece.astype(jnp.bfloat16)

    span = min(128, own)
    for first in range(0, own, ROWS):
        if first % span == 0:
            here = slice(first * groups, (first + span) * groups)
            lags = dets * LANES
            mixed_a = jnp.dot(hankel[here, :], weights[0, :lags, :], preferred_element_type=jnp.float32)
            mixed_b = jnp.dot(
                hankel[here, : lags - LANES], weights[0, lags:, :], preferred_element_type=jnp.float32
            )
        best = None
        for k in range(copies * temps):
            place = first % span * groups + 2 * k * ROWS
            power = None
            for mixed in (mixed_a, mixed_b):
                for part in (mixed[place : place + ROWS], mixed[place + ROWS : place + 2 * ROWS]):
                    power = part * part if power is None else power + part * part
            best = power if best is None else jnp.maximum(best, power)
        out[first : first + ROWS, :] = best


def body(strain, templates, lengths, antenna, delays):
    devices = lax.axis_size("filt")
    copies = lax.axis_size("sky")
    temps, dets, bins = templates.shape[1], strain.shape[1], strain.shape[2]
    sky = delays.shape[1]
    depth = N2
    rows = bins // depth
    whole_length = 2 * bins * devices
    own = N1 // devices
    span = N1 + 2 * DM
    half_tiles = -(-span // (2 * LANES))
    width = -(-own // LANES) * LANES + LANES
    tabs = tables(depth, rows, whole_length, half_tiles, devices)
    start, col_first, col_step, row_first, row_step, offset = (jnp.asarray(t) for t in tabs[:6])
    flip = jnp.asarray(tabs[6], jnp.bfloat16)
    count = temps * dets
    vmem = pl.BlockSpec(memory_space=pltpu.VMEM)
    smem = pl.BlockSpec(memory_space=pltpu.SMEM)
    shaped_s = strain.reshape(2, dets, rows, depth)
    shaped_h = templates.reshape(2, temps, rows, depth)
    parts = pl.pallas_call(
        functools.partial(series_kernel, temps, dets, own, devices, copies, half_tiles, 1),
        out_shape=jax.ShapeDtypeStruct((devices * copies, ROWS, width), jnp.bfloat16),
        in_specs=[smem] + [vmem] * 9,
        out_specs=vmem,
        scratch_shapes=[
            pltpu.VMEM((2 * count * rows, depth), jnp.bfloat16),
            pltpu.VMEM((2, depth, LANES), jnp.float32),
            pltpu.VMEM((2, rows, LANES), jnp.float32),
            pltpu.VMEM((ROWS, 2 * half_tiles * LANES), jnp.bfloat16),
        ],
        compiler_params=pltpu.CompilerParams(vmem_limit_bytes=40 << 20),
        name="series",
    )(lengths, shaped_s, shaped_h, start, col_first, col_step, row_first, row_step, offset, flip)
    received = lax.all_to_all(parts, ("filt", "sky"), split_axis=0, concat_axis=0, tiled=True)
    tile = 4 * LANES if sky % (4 * LANES) == 0 else 2 * LANES
    weights = pl.pallas_call(
        functools.partial(weight_kernel, dets, tile),
        out_shape=jax.ShapeDtypeStruct((sky // tile, (2 * dets - 1) * LANES, tile), jnp.bfloat16),
        in_specs=[vmem] * 2,
        out_specs=vmem,
        compiler_params=pltpu.CompilerParams(vmem_limit_bytes=16 << 20),
        cost_estimate=pl.CostEstimate(flops=1 << 22, bytes_accessed=3 << 20, transcendentals=0),
        name="weights",
    )(delays, antenna)
    best = pl.pallas_call(
        functools.partial(sky_kernel, temps, dets, own, devices, copies),
        out_shape=jax.ShapeDtypeStruct((own, sky), jnp.float32),
        grid=(sky // tile,),
        in_specs=[vmem, pl.BlockSpec((1, (2 * dets - 1) * LANES, tile), lambda i: (i, 0, 0))],
        out_specs=pl.BlockSpec((own, tile), lambda i: (0, i)),
        scratch_shapes=[pltpu.VMEM((copies * temps * 2 * own, dets * LANES), jnp.bfloat16)],
        compiler_params=pltpu.CompilerParams(vmem_limit_bytes=24 << 20),
        name="sky",
    )(received, weights)
    return best[None]


def solution(mesh):
    in_specs = (
        P(None, "grp", "filt"),
        P(None, "sky", "filt"),
        P("sky"),
        P(None, None, "sky"),
        P(None, "sky"),
    )
    out_specs = P("grp", "filt", "sky")
    return jax.shard_map(body, mesh=mesh, in_specs=in_specs, out_specs=out_specs, check_vma=False)
```

```python
import functools

import jax
import jax.numpy as jnp
import numpy as np
from jax import lax
from jax.experimental import pallas as pl
from jax.experimental.pallas import tpu as pltpu
from jax.sharding import PartitionSpec as P

N1 = 2048
N2 = 512
DM = 48
K2 = 3
LANES = 128
ROWS = 16


def turn(phase):
    angle = 2.0 * np.pi * (phase - np.floor(phase))
    return np.stack([np.cos(angle), np.sin(angle)]).astype(np.float32)


def tables(depth, rows, whole_length, half_tiles, devices):
    centre2 = 2 * (2 * N1 + DM) - 2 * half_tiles * LANES - 1
    row = np.arange(rows, dtype=np.int64)[:, None]
    col = np.arange(depth, dtype=np.int64)[None, :]
    odd = 2 * np.arange(2 * LANES, dtype=np.int64)[None, :] + 1
    pair = 2 * np.arange(depth // 2, dtype=np.int64)[:, None] + 1
    middle = 2 * row * depth + depth - 1
    step = 4 * LANES * np.ones((1, 2 * LANES), np.int64)
    turns = 4 * whole_length
    start = turn(((row * depth + col) * (2 * centre2) % turns) / turns)
    start = np.concatenate([start[:, :, depth // 2 :], start[:, :, : depth // 2][:, :, ::-1]])
    col_first = turn((pair * odd % turns) / turns)
    col_step = turn((pair * step % turns) / turns)
    row_first = turn((middle * odd % turns) / turns)
    row_step = turn((middle * step % turns) / turns)
    odd = odd[:, :LANES]
    pos = np.arange(devices, dtype=np.int64)[:, None]
    t_up = (centre2 + odd) // 2
    t_down = (centre2 - odd) // 2
    base = rows * depth
    up = turn((pos * base * t_up % whole_length) / whole_length)
    down = turn((pos * base * t_down % whole_length) / whole_length)
    offset = np.concatenate([up, down]).transpose(1, 0, 2)
    flip = np.eye(2 * LANES, dtype=np.float32)[::-1]
    return start, col_first, col_step, row_first, row_step, offset, flip


def series_kernel(
    temps, dets, own, devices, copies, half_tiles,
    lengths, strain, templates, start, col_first, col_step, row_first, row_step, offset, flip,
    out, even, odd, back_s, back_h, col_now, row_now, series,
):
    rows, depth = strain.shape[2], strain.shape[3]
    side = depth // 2
    count = temps * dets
    pos = lax.axis_index("filt")
    for r in range(2):
        for d in range(dets):
            turned = jnp.dot(strain[r, d, :, :side], flip[...], preferred_element_type=jnp.float32)
            back_s[r, d] = turned.astype(jnp.bfloat16)
        for k in range(temps):
            turned = jnp.dot(templates[r, k, :, :side], flip[...], preferred_element_type=jnp.float32)
            back_h[r, k] = turned.astype(jnp.bfloat16)
    norms = [jnp.zeros((ROWS, side), jnp.float32) for _ in range(temps)]

    def filter_chunk(step, norms):
        first = pl.multiple_of(step * ROWS, ROWS)
        here = pl.ds(first, ROWS)
        row_bin = (pos * rows + first) * depth + lax.broadcasted_iota(jnp.int32, (ROWS, side), 0) * depth
        lane = lax.broadcasted_iota(jnp.int32, (ROWS, side), 1)
        bins = (row_bin + side + lane, row_bin + side - 1 - lane)
        s_re = [(strain[0, d, here, side:].astype(jnp.float32), back_s[0, d, here, :].astype(jnp.float32)) for d in range(dets)]
        s_im = [(strain[1, d, here, side:].astype(jnp.float32), back_s[1, d, here, :].astype(jnp.float32)) for d in range(dets)]
        added = []
        for k in range(temps):
            energy = norms[k]
            h_all = (
                (templates[0, k, here, side:], templates[1, k, here, side:]),
                (back_h[0, k, here, :], back_h[1, k, here, :]),
            )
            g = []
            for i in range(2):
                inside = bins[i] < lengths[k]
                h_re = jnp.where(inside, h_all[i][0].astype(jnp.float32), 0.0)
                h_im = jnp.where(inside, h_all[i][1].astype(jnp.float32), 0.0)
                energy = energy + (h_re * h_re + h_im * h_im)
                p_re, p_im = start[2 * i, here, :], start[2 * i + 1, here, :]
                g.append((h_re * p_re + h_im * p_im, h_re * p_im - h_im * p_re))
            added.append(energy)
            for d in range(dets):
                place = 2 * ((k * dets + d) * rows + first)
                x_re = [g[i][0] * s_re[d][i] - g[i][1] * s_im[d][i] for i in range(2)]
                x_im = [g[i][0] * s_im[d][i] + g[i][1] * s_re[d][i] for i in range(2)]
                at_re = pl.ds(pl.multiple_of(place, ROWS), ROWS)
                at_im = pl.ds(pl.multiple_of(place + ROWS, ROWS), ROWS)
                even[at_re, :] = (x_re[0] + x_re[1]).astype(jnp.bfloat16)
                even[at_im, :] = (x_im[0] + x_im[1]).astype(jnp.bfloat16)
                odd[at_re, :] = (x_re[0] - x_re[1]).astype(jnp.bfloat16)
                odd[at_im, :] = (x_im[0] - x_im[1]).astype(jnp.bfloat16)
        return added

    norms = lax.fori_loop(0, rows // ROWS, filter_chunk, norms)
    col_now[...] = col_first[...]
    row_now[...] = row_first[...]

    def section(tile, tiles, last):
        wide = tiles * LANES
        high, low = [], []
        for k in range(temps):
            total = jnp.sum(jnp.sum(norms[k], axis=0, keepdims=True), axis=1, keepdims=True)
            total = jnp.broadcast_to(total, (1, wide))
            first = total.astype(jnp.bfloat16).astype(jnp.float32)
            high.append(first)
            low.append(total - first)
        f_ur, f_ui, f_dr, f_di = (
            jnp.concatenate([offset[pos, i : i + 1, :]] * tiles, axis=1) for i in range(4)
        )
        c_re, c_im = col_now[0], col_now[1]
        cos, sin = c_re[:, :wide].astype(jnp.bfloat16), c_im[:, :wide].astype(jnp.bfloat16)
        if not last:
            d_re, d_im = col_step[0], col_step[1]
            col_now[0] = c_re * d_re - c_im * d_im
            col_now[1] = c_re * d_im + c_im * d_re
        on_even = jnp.dot(even[...], cos, preferred_element_type=jnp.float32)
        on_odd = jnp.dot(odd[...], sin, preferred_element_type=jnp.float32)
        up_re, up_im, down_re, down_im = [], [], [], []
        for q in range(count):
            s1 = s2 = s3 = s4 = None
            for block in range(0, rows, ROWS):
                for half in range(0, ROWS, 8):
                    w_re = row_now[0, block + half : block + half + 8, :wide]
                    w_im = row_now[1, block + half : block + half + 8, :wide]
                    top = 2 * (q * rows + block) + half
                    end = top + ROWS
                    a, e = on_even[top : top + 8], on_even[end : end + 8]
                    d, b = on_odd[top : top + 8], on_odd[end : end + 8]
                    n1, n2 = a * w_re - d * w_im, b * w_re + e * w_im
                    n3, n4 = e * w_re - b * w_im, d * w_re + a * w_im
                    s1 = n1 if s1 is None else s1 + n1
                    s2 = n2 if s2 is None else s2 + n2
                    s3 = n3 if s3 is None else s3 + n3
                    s4 = n4 if s4 is None else s4 + n4
            r = jnp.sum(s1 - s2, axis=0, keepdims=True)
            i = jnp.sum(s3 + s4, axis=0, keepdims=True)
            up_re.append(r * f_ur - i * f_ui)
            up_im.append(r * f_ui + i * f_ur)
            r = jnp.sum(s1 + s2, axis=0, keepdims=True)
            i = jnp.sum(s3 - s4, axis=0, keepdims=True)
            down_re.append(r * f_dr - i * f_di)
            down_im.append(r * f_di + i * f_dr)
        upper = jnp.concatenate(up_re + high + up_im + low, axis=0).astype(jnp.bfloat16)
        lower = jnp.concatenate(down_re + high + down_im + low, axis=0).astype(jnp.bfloat16)
        turned = flip[2 * LANES - wide :, :wide]
        upper = jnp.dot(upper, turned, preferred_element_type=jnp.float32).astype(jnp.bfloat16)
        series[:, pl.ds(pl.multiple_of((half_tiles - tiles - tile) * LANES, LANES), wide)] = upper
        series[:, pl.ds(pl.multiple_of((half_tiles + tile) * LANES, LANES), wide)] = lower
        if not last:
            w_re, w_im = row_now[0], row_now[1]
            d_re, d_im = row_step[0], row_step[1]
            row_now[0] = w_re * d_re - w_im * d_im
            row_now[1] = w_re * d_im + w_im * d_re

    def some(step, carry):
        section(2 * step, 2, False)
        return carry

    lax.fori_loop(0, half_tiles // 2, some, 0)
    if half_tiles % 2:
        section(half_tiles - 1, 1, True)

    width = out.shape[2]
    for target in range(devices):
        first = own * (devices - 1 - target)
        window = series[:, first : first + width]
        for copy in range(copies):
            out[target * copies + copy] = window


def weight_kernel(dets, tile, delays, antenna, weights):
    sky = delays.shape[1]
    lag = DM - lax.broadcasted_iota(jnp.int32, (LANES, tile), 0)
    for i in range(sky // tile):
        part = slice(i * tile, (i + 1) * tile)
        rows = [[antenna[p, d : d + 1, part].astype(jnp.float32) for d in range(dets)] for p in range(2)]
        x, y = rows[0][-1], rows[1][-1]
        most = jnp.maximum(jnp.abs(x), jnp.abs(y))
        some = most > 0.0
        least = jnp.where(some, most, 1.0)
        x, y = jnp.where(some, x / least, 1.0), jnp.where(some, y / least, 0.0)
        unit = lax.rsqrt(x * x + y * y)
        cos, sin = x * unit, y * unit
        first = [cos * rows[0][d] + sin * rows[1][d] for d in range(dets)]
        second = [cos * rows[1][d] - sin * rows[0][d] for d in range(dets - 1)]
        for d in range(dets):
            hit = lag == delays[d : d + 1, part]
            weights[i, d * LANES : (d + 1) * LANES, :] = jnp.where(hit, first[d], 0.0).astype(jnp.bfloat16)
            if d < dets - 1:
                place = (dets + d) * LANES
                weights[i, place : place + LANES, :] = jnp.where(hit, second[d], 0.0).astype(jnp.bfloat16)


def sky_kernel(temps, dets, own, sources, copies, received, weights, out, hankel):
    width = received.shape[2]
    count = temps * dets
    blocks = -(-own // LANES)
    groups = 2 * copies * temps

    @pl.when(pl.program_id(0) == 0)
    def _():
        for c in range(copies):
            total = received[c].astype(jnp.float32)
            for source in range(1, sources):
                total = total + received[source * copies + c].astype(jnp.float32)
            half = ROWS // 2
            for k in range(temps):
                norm = total[count + k : count + k + 1] + total[half + count + k : half + count + k + 1]
                scale = lax.rsqrt(norm + 1e-06)
                lines = []
                for part in range(2):
                    for d in range(dets):
                        row = part * half + k * dets + d
                        line = (total[row : row + 1] * scale).astype(jnp.bfloat16).astype(jnp.float32)
                        lines.append(
                            pltpu.roll(jnp.broadcast_to(line, (8, width)), 0, 1, stride=1, stride_axis=0)
                        )
                base = jnp.concatenate(lines, axis=0)
                for first in range(0, min(own, LANES), ROWS):
                    moved = [
                        pltpu.roll(base, (t + 1 - own + (blocks - 1) * LANES) % width, 1) for t in (first, first + 8)
                    ]
                    for part in range(2):
                        group = 2 * (c * temps + k) + part
                        for d in range(dets):
                            row = 8 * (part * dets + d)
                            for block in range(blocks):
                                lane = (blocks - 1 - block) * LANES
                                piece = jnp.concatenate([m[row : row + 8, lane : lane + LANES] for m in moved], axis=0)
                                place = ((block * LANES + first) // ROWS * groups + group) * ROWS
                                hankel[place : place + ROWS, d * LANES : (d + 1) * LANES] = piece.astype(jnp.bfloat16)

    span = min(128, own)
    for first in range(0, own, ROWS):
        if first % span == 0:
            here = slice(first * groups, (first + span) * groups)
            lags = dets * LANES
            mixed_a = jnp.dot(hankel[here, :], weights[0, :lags, :], preferred_element_type=jnp.float32)
            mixed_b = jnp.dot(
                hankel[here, : lags - LANES], weights[0, lags:, :], preferred_element_type=jnp.float32
            )
        best = None
        for k in range(copies * temps):
            place = first % span * groups + 2 * k * ROWS
            power = None
            for mixed in (mixed_a, mixed_b):
                for part in (mixed[place : place + ROWS], mixed[place + ROWS : place + 2 * ROWS]):
                    power = part * part if power is None else power + part * part
            best = power if best is None else jnp.maximum(best, power)
        out[first : first + ROWS, :] = best


def body(strain, templates, lengths, antenna, delays):
    devices = lax.axis_size("filt")
    copies = lax.axis_size("sky")
    temps, dets, bins = templates.shape[1], strain.shape[1], strain.shape[2]
    sky = delays.shape[1]
    depth = 4 * LANES
    rows = bins // depth
    whole_length = 2 * bins * devices
    own = N1 // devices
    span = N1 + 2 * DM
    half_tiles = -(-span // (2 * LANES))
    width = -(-own // LANES) * LANES + LANES
    tabs = tables(depth, rows, whole_length, half_tiles, devices)
    start, col_first, col_step, row_first, row_step, offset = (jnp.asarray(t) for t in tabs[:6])
    flip = jnp.asarray(tabs[6], jnp.bfloat16)
    count = temps * dets
    vmem = pl.BlockSpec(memory_space=pltpu.VMEM)
    smem = pl.BlockSpec(memory_space=pltpu.SMEM)
    shaped_s = strain.reshape(2, dets, rows, depth)
    shaped_h = templates.reshape(2, temps, rows, depth)
    parts = pl.pallas_call(
        functools.partial(series_kernel, temps, dets, own, devices, copies, half_tiles),
        out_shape=jax.ShapeDtypeStruct((devices * copies, ROWS, width), jnp.bfloat16),
        in_specs=[smem] + [vmem] * 9,
        out_specs=vmem,
        scratch_shapes=[
            pltpu.VMEM((2 * count * rows, depth // 2), jnp.bfloat16),
            pltpu.VMEM((2 * count * rows, depth // 2), jnp.bfloat16),
            pltpu.VMEM((2, dets, rows, depth // 2), jnp.bfloat16),
            pltpu.VMEM((2, temps, rows, depth // 2), jnp.bfloat16),
            pltpu.VMEM((2, depth // 2, 2 * LANES), jnp.float32),
            pltpu.VMEM((2, rows, 2 * LANES), jnp.float32),
            pltpu.VMEM((ROWS, 2 * half_tiles * LANES), jnp.bfloat16),
        ],
        compiler_params=pltpu.CompilerParams(vmem_limit_bytes=40 << 20),
        name="series",
    )(lengths, shaped_s, shaped_h, start, col_first, col_step, row_first, row_step, offset, flip)
    received = lax.all_to_all(parts, ("filt", "sky"), split_axis=0, concat_axis=0, tiled=True)
    tile = 4 * LANES if sky % (4 * LANES) == 0 else 2 * LANES
    weights = pl.pallas_call(
        functools.partial(weight_kernel, dets, tile),
        out_shape=jax.ShapeDtypeStruct((sky // tile, (2 * dets - 1) * LANES, tile), jnp.bfloat16),
        in_specs=[vmem] * 2,
        out_specs=vmem,
        compiler_params=pltpu.CompilerParams(vmem_limit_bytes=16 << 20),
        cost_estimate=pl.CostEstimate(flops=1 << 22, bytes_accessed=3 << 20, transcendentals=0),
        name="weights",
    )(delays, antenna)
    best = pl.pallas_call(
        functools.partial(sky_kernel, temps, dets, own, devices, copies),
        out_shape=jax.ShapeDtypeStruct((own, sky), jnp.float32),
        grid=(sky // tile,),
        in_specs=[vmem, pl.BlockSpec((1, (2 * dets - 1) * LANES, tile), lambda i: (i, 0, 0))],
        out_specs=pl.BlockSpec((own, tile), lambda i: (0, i)),
        scratch_shapes=[pltpu.VMEM((copies * temps * 2 * own, dets * LANES), jnp.bfloat16)],
        compiler_params=pltpu.CompilerParams(vmem_limit_bytes=24 << 20),
        name="sky",
    )(received, weights)
    return best[None]


def solution(mesh):
    in_specs = (
        P(None, "grp", "filt"),
        P(None, "sky", "filt"),
        P("sky"),
        P(None, None, "sky"),
        P(None, "sky"),
    )
    out_specs = P("grp", "filt", "sky")
    return jax.shard_map(body, mesh=mesh, in_specs=in_specs, out_specs=out_specs, check_vma=False)
```

```python
import functools

import jax
import jax.numpy as jnp
import numpy as np
from jax import lax
from jax.experimental import pallas as pl
from jax.experimental.pallas import tpu as pltpu
from jax.sharding import PartitionSpec as P

N1 = 2048
N2 = 512
DM = 48
K2 = 3
LANES = 128
ROWS = 16


def turn(phase):
    angle = 2.0 * np.pi * (phase - np.floor(phase))
    return np.stack([np.cos(angle), np.sin(angle)]).astype(np.float32)


def tables(depth, rows, whole_length, half_tiles, devices):
    centre2 = 2 * (2 * N1 + DM) - 2 * half_tiles * LANES - 1
    row = np.arange(rows, dtype=np.int64)[:, None]
    col = np.arange(depth, dtype=np.int64)[None, :]
    odd = 2 * np.arange(2 * LANES, dtype=np.int64)[None, :] + 1
    pair = 2 * np.arange(depth // 2, dtype=np.int64)[:, None] + 1
    middle = 2 * row * depth + depth - 1
    step = 4 * LANES * np.ones((1, 2 * LANES), np.int64)
    turns = 4 * whole_length
    start = turn(((row * depth + col) * (2 * centre2) % turns) / turns)
    start = np.concatenate([start[:, :, depth // 2 :], start[:, :, : depth // 2][:, :, ::-1]])
    col_first = turn((pair * odd % turns) / turns)
    col_step = turn((pair * step % turns) / turns)
    row_first = turn((middle * odd % turns) / turns)
    row_step = turn((middle * step % turns) / turns)
    odd = odd[:, :LANES]
    pos = np.arange(devices, dtype=np.int64)[:, None]
    t_up = (centre2 + odd) // 2
    t_down = (centre2 - odd) // 2
    base = rows * depth
    up = turn((pos * base * t_up % whole_length) / whole_length)
    down = turn((pos * base * t_down % whole_length) / whole_length)
    offset = np.concatenate([up, down]).transpose(1, 0, 2)
    flip = np.eye(2 * LANES, dtype=np.float32)[::-1]
    return start, col_first, col_step, row_first, row_step, offset, flip


def series_kernel(
    temps, dets, own, devices, copies, half_tiles,
    lengths, strain, templates, start, col_first, col_step, row_first, row_step, offset, flip,
    out, even, odd, back_s, back_h, col_now, row_now, series,
):
    rows, depth = strain.shape[2], strain.shape[3]
    side = depth // 2
    count = temps * dets
    pos = lax.axis_index("filt")
    for r in range(2):
        for d in range(dets):
            turned = jnp.dot(strain[d, r, :, :side], flip[...], preferred_element_type=jnp.float32)
            back_s[r, d] = turned.astype(jnp.bfloat16)
        for k in range(temps):
            turned = jnp.dot(templates[r, k, :, :side], flip[...], preferred_element_type=jnp.float32)
            back_h[r, k] = turned.astype(jnp.bfloat16)
    norms = [jnp.zeros((ROWS, side), jnp.float32) for _ in range(temps)]

    def filter_chunk(step, norms):
        first = pl.multiple_of(step * ROWS, ROWS)
        here = pl.ds(first, ROWS)
        row_bin = (pos * rows + first) * depth + lax.broadcasted_iota(jnp.int32, (ROWS, side), 0) * depth
        lane = lax.broadcasted_iota(jnp.int32, (ROWS, side), 1)
        bins = (row_bin + side + lane, row_bin + side - 1 - lane)
        s_re = [(strain[d, 0, here, side:].astype(jnp.float32), back_s[0, d, here, :].astype(jnp.float32)) for d in range(dets)]
        s_im = [(strain[d, 1, here, side:].astype(jnp.float32), back_s[1, d, here, :].astype(jnp.float32)) for d in range(dets)]
        added = []
        for k in range(temps):
            energy = norms[k]
            h_all = (
                (templates[0, k, here, side:], templates[1, k, here, side:]),
                (back_h[0, k, here, :], back_h[1, k, here, :]),
            )
            g = []
            for i in range(2):
                inside = bins[i] < lengths[k]
                h_re = jnp.where(inside, h_all[i][0].astype(jnp.float32), 0.0)
                h_im = jnp.where(inside, h_all[i][1].astype(jnp.float32), 0.0)
                energy = energy + (h_re * h_re + h_im * h_im)
                p_re, p_im = start[2 * i, here, :], start[2 * i + 1, here, :]
                g.append((h_re * p_re + h_im * p_im, h_re * p_im - h_im * p_re))
            added.append(energy)
            for d in range(dets):
                place = 2 * ((k * dets + d) * rows + first)
                x_re = [g[i][0] * s_re[d][i] - g[i][1] * s_im[d][i] for i in range(2)]
                x_im = [g[i][0] * s_im[d][i] + g[i][1] * s_re[d][i] for i in range(2)]
                at_re = pl.ds(pl.multiple_of(place, ROWS), ROWS)
                at_im = pl.ds(pl.multiple_of(place + ROWS, ROWS), ROWS)
                even[at_re, :] = (x_re[0] + x_re[1]).astype(jnp.bfloat16)
                even[at_im, :] = (x_im[0] + x_im[1]).astype(jnp.bfloat16)
                odd[at_re, :] = (x_re[0] - x_re[1]).astype(jnp.bfloat16)
                odd[at_im, :] = (x_im[0] - x_im[1]).astype(jnp.bfloat16)
        return added

    norms = lax.fori_loop(0, rows // ROWS, filter_chunk, norms)
    col_now[...] = col_first[...]
    row_now[...] = row_first[...]

    def section(tile, tiles, last):
        wide = tiles * LANES
        high, low = [], []
        for k in range(temps):
            total = jnp.sum(jnp.sum(norms[k], axis=0, keepdims=True), axis=1, keepdims=True)
            total = jnp.broadcast_to(total, (1, wide))
            first = total.astype(jnp.bfloat16).astype(jnp.float32)
            high.append(first)
            low.append(total - first)
        f_ur, f_ui, f_dr, f_di = (
            jnp.concatenate([offset[pos, i : i + 1, :]] * tiles, axis=1) for i in range(4)
        )
        c_re, c_im = col_now[0], col_now[1]
        cos, sin = c_re[:, :wide].astype(jnp.bfloat16), c_im[:, :wide].astype(jnp.bfloat16)
        if not last:
            d_re, d_im = col_step[0], col_step[1]
            col_now[0] = c_re * d_re - c_im * d_im
            col_now[1] = c_re * d_im + c_im * d_re
        on_even = jnp.dot(even[...], cos, preferred_element_type=jnp.float32)
        on_odd = jnp.dot(odd[...], sin, preferred_element_type=jnp.float32)
        up_re, up_im, down_re, down_im = [], [], [], []
        for q in range(count):
            s1 = s2 = s3 = s4 = None
            for block in range(0, rows, ROWS):
                for half in range(0, ROWS, 8):
                    w_re = row_now[0, block + half : block + half + 8, :wide]
                    w_im = row_now[1, block + half : block + half + 8, :wide]
                    top = 2 * (q * rows + block) + half
                    end = top + ROWS
                    a, e = on_even[top : top + 8], on_even[end : end + 8]
                    d, b = on_odd[top : top + 8], on_odd[end : end + 8]
                    n1, n2 = a * w_re - d * w_im, b * w_re + e * w_im
                    n3, n4 = e * w_re - b * w_im, d * w_re + a * w_im
                    s1 = n1 if s1 is None else s1 + n1
                    s2 = n2 if s2 is None else s2 + n2
                    s3 = n3 if s3 is None else s3 + n3
                    s4 = n4 if s4 is None else s4 + n4
            r = jnp.sum(s1 - s2, axis=0, keepdims=True)
            i = jnp.sum(s3 + s4, axis=0, keepdims=True)
            up_re.append(r * f_ur - i * f_ui)
            up_im.append(r * f_ui + i * f_ur)
            r = jnp.sum(s1 + s2, axis=0, keepdims=True)
            i = jnp.sum(s3 - s4, axis=0, keepdims=True)
            down_re.append(r * f_dr - i * f_di)
            down_im.append(r * f_di + i * f_dr)
        upper = jnp.concatenate(up_re + high + up_im + low, axis=0).astype(jnp.bfloat16)
        lower = jnp.concatenate(down_re + high + down_im + low, axis=0).astype(jnp.bfloat16)
        turned = flip[2 * LANES - wide :, :wide]
        upper = jnp.dot(upper, turned, preferred_element_type=jnp.float32).astype(jnp.bfloat16)
        series[:, pl.ds(pl.multiple_of((half_tiles - tiles - tile) * LANES, LANES), wide)] = upper
        series[:, pl.ds(pl.multiple_of((half_tiles + tile) * LANES, LANES), wide)] = lower
        if not last:
            w_re, w_im = row_now[0], row_now[1]
            d_re, d_im = row_step[0], row_step[1]
            row_now[0] = w_re * d_re - w_im * d_im
            row_now[1] = w_re * d_im + w_im * d_re

    def some(step, carry):
        section(2 * step, 2, False)
        return carry

    lax.fori_loop(0, half_tiles // 2, some, 0)
    if half_tiles % 2:
        section(half_tiles - 1, 1, True)

    width = out.shape[2]
    for target in range(devices):
        first = own * (devices - 1 - target)
        window = series[:, first : first + width]
        for copy in range(copies):
            out[target * copies + copy] = window


def weight_kernel(dets, tile, delays, antenna, weights):
    sky = delays.shape[1]
    lag = DM - lax.broadcasted_iota(jnp.int32, (LANES, tile), 0)
    for i in range(sky // tile):
        part = slice(i * tile, (i + 1) * tile)
        rows = [[antenna[p, d : d + 1, part].astype(jnp.float32) for d in range(dets)] for p in range(2)]
        x, y = rows[0][-1], rows[1][-1]
        most = jnp.maximum(jnp.abs(x), jnp.abs(y))
        some = most > 0.0
        least = jnp.where(some, most, 1.0)
        x, y = jnp.where(some, x / least, 1.0), jnp.where(some, y / least, 0.0)
        unit = lax.rsqrt(x * x + y * y)
        cos, sin = x * unit, y * unit
        first = [cos * rows[0][d] + sin * rows[1][d] for d in range(dets)]
        second = [cos * rows[1][d] - sin * rows[0][d] for d in range(dets - 1)]
        for d in range(dets):
            hit = lag == delays[d : d + 1, part]
            weights[i, d * LANES : (d + 1) * LANES, :] = jnp.where(hit, first[d], 0.0).astype(jnp.bfloat16)
            if d < dets - 1:
                place = (dets + d) * LANES
                weights[i, place : place + LANES, :] = jnp.where(hit, second[d], 0.0).astype(jnp.bfloat16)


def sky_kernel(temps, dets, own, sources, copies, received, weights, out, hankel):
    width = received.shape[2]
    count = temps * dets
    blocks = -(-own // LANES)
    groups = 2 * copies * temps

    @pl.when(pl.program_id(0) == 0)
    def _():
        for c in range(copies):
            total = received[c].astype(jnp.float32)
            for source in range(1, sources):
                total = total + received[source * copies + c].astype(jnp.float32)
            half = ROWS // 2
            for k in range(temps):
                norm = total[count + k : count + k + 1] + total[half + count + k : half + count + k + 1]
                scale = lax.rsqrt(norm + 1e-06)
                lines = []
                for part in range(2):
                    for d in range(dets):
                        row = part * half + k * dets + d
                        line = (total[row : row + 1] * scale).astype(jnp.bfloat16).astype(jnp.float32)
                        lines.append(
                            pltpu.roll(jnp.broadcast_to(line, (8, width)), 0, 1, stride=1, stride_axis=0)
                        )
                base = jnp.concatenate(lines, axis=0)
                for first in range(0, min(own, LANES), ROWS):
                    moved = [
                        pltpu.roll(base, (t + 1 - own + (blocks - 1) * LANES) % width, 1) for t in (first, first + 8)
                    ]
                    for part in range(2):
                        group = 2 * (c * temps + k) + part
                        for d in range(dets):
                            row = 8 * (part * dets + d)
                            for block in range(blocks):
                                lane = (blocks - 1 - block) * LANES
                                piece = jnp.concatenate([m[row : row + 8, lane : lane + LANES] for m in moved], axis=0)
                                place = ((block * LANES + first) // ROWS * groups + group) * ROWS
                                hankel[place : place + ROWS, d * LANES : (d + 1) * LANES] = piece.astype(jnp.bfloat16)

    span = min(128, own)
    for first in range(0, own, ROWS):
        if first % span == 0:
            here = slice(first * groups, (first + span) * groups)
            lags = dets * LANES
            mixed_a = jnp.dot(hankel[here, :], weights[0, :lags, :], preferred_element_type=jnp.float32)
            mixed_b = jnp.dot(
                hankel[here, : lags - LANES], weights[0, lags:, :], preferred_element_type=jnp.float32
            )
        best = None
        for k in range(copies * temps):
            place = first % span * groups + 2 * k * ROWS
            power = None
            for mixed in (mixed_a, mixed_b):
                for part in (mixed[place : place + ROWS], mixed[place + ROWS : place + 2 * ROWS]):
                    power = part * part if power is None else power + part * part
            best = power if best is None else jnp.maximum(best, power)
        out[first : first + ROWS, :] = best


def body(strain, templates, lengths, antenna, delays):
    devices = lax.axis_size("filt")
    copies = lax.axis_size("sky")
    temps, dets, bins = templates.shape[1], strain.shape[1], strain.shape[2]
    sky = delays.shape[1]
    depth = 4 * LANES
    rows = bins // depth
    whole_length = 2 * bins * devices
    own = N1 // devices
    span = N1 + 2 * DM
    half_tiles = -(-span // (2 * LANES))
    width = -(-own // LANES) * LANES + LANES
    tabs = tables(depth, rows, whole_length, half_tiles, devices)
    start, col_first, col_step, row_first, row_step, offset = (jnp.asarray(t) for t in tabs[:6])
    flip = jnp.asarray(tabs[6], jnp.bfloat16)
    count = temps * dets
    vmem = pl.BlockSpec(memory_space=pltpu.VMEM)
    smem = pl.BlockSpec(memory_space=pltpu.SMEM)
    shaped_s = strain.reshape(2, dets, rows, depth).transpose(1, 0, 2, 3)
    shaped_h = templates.reshape(2, temps, rows, depth)
    parts = pl.pallas_call(
        functools.partial(series_kernel, temps, dets, own, devices, copies, half_tiles),
        out_shape=jax.ShapeDtypeStruct((devices * copies, ROWS, width), jnp.bfloat16),
        in_specs=[smem] + [vmem] * 9,
        out_specs=vmem,
        scratch_shapes=[
            pltpu.VMEM((2 * count * rows, depth // 2), jnp.bfloat16),
            pltpu.VMEM((2 * count * rows, depth // 2), jnp.bfloat16),
            pltpu.VMEM((2, dets, rows, depth // 2), jnp.bfloat16),
            pltpu.VMEM((2, temps, rows, depth // 2), jnp.bfloat16),
            pltpu.VMEM((2, depth // 2, 2 * LANES), jnp.float32),
            pltpu.VMEM((2, rows, 2 * LANES), jnp.float32),
            pltpu.VMEM((ROWS, 2 * half_tiles * LANES), jnp.bfloat16),
        ],
        compiler_params=pltpu.CompilerParams(vmem_limit_bytes=40 << 20),
        name="series",
    )(lengths, shaped_s, shaped_h, start, col_first, col_step, row_first, row_step, offset, flip)
    received = lax.all_to_all(parts, ("filt", "sky"), split_axis=0, concat_axis=0, tiled=True)
    tile = 4 * LANES if sky % (4 * LANES) == 0 else 2 * LANES
    weights = pl.pallas_call(
        functools.partial(weight_kernel, dets, tile),
        out_shape=jax.ShapeDtypeStruct((sky // tile, (2 * dets - 1) * LANES, tile), jnp.bfloat16),
        in_specs=[vmem] * 2,
        out_specs=vmem,
        compiler_params=pltpu.CompilerParams(vmem_limit_bytes=16 << 20),
        cost_estimate=pl.CostEstimate(flops=1 << 22, bytes_accessed=3 << 20, transcendentals=0),
        name="weights",
    )(delays, antenna)
    best = pl.pallas_call(
        functools.partial(sky_kernel, temps, dets, own, devices, copies),
        out_shape=jax.ShapeDtypeStruct((own, sky), jnp.float32),
        grid=(sky // tile,),
        in_specs=[vmem, pl.BlockSpec((1, (2 * dets - 1) * LANES, tile), lambda i: (i, 0, 0))],
        out_specs=pl.BlockSpec((own, tile), lambda i: (0, i)),
        scratch_shapes=[pltpu.VMEM((copies * temps * 2 * own, dets * LANES), jnp.bfloat16)],
        compiler_params=pltpu.CompilerParams(vmem_limit_bytes=24 << 20),
        name="sky",
    )(received, weights)
    return best[None]


def solution(mesh):
    in_specs = (
        P(None, "grp", "filt"),
        P(None, "sky", "filt"),
        P("sky"),
        P(None, None, "sky"),
        P(None, "sky"),
    )
    out_specs = P("grp", "filt", "sky")
    return jax.shard_map(body, mesh=mesh, in_specs=in_specs, out_specs=out_specs, check_vma=False)
```
